512 devices in a mesh: ctx: 32 (over z_hi, x, core), section: 16 (over y, z_lo).
Axes of the slice: x: 4, y: 8, z: 8 (z_hi: 4, z_lo: 2; z = z_hi * 2 + z_lo), core: 2. Of those that a mesh axis runs over, the one named last changes fastest.
Arguments:
- queries: bfloat16 [16, 8192, 2048], P('section', 'ctx'), may hold values from -9 to 9
- keys: bfloat16 [16, 8192, 2048], P('section', 'ctx'), may hold values from -9 to 9
- values: bfloat16 [16, 8192, 2048], P('section', 'ctx'), may hold values from -6 to 6
- segments: int32 [16, 8192], replicated, may hold values from 0 to 1, as said below
- gain_query: bfloat16 [16, 2048], P('section'), may hold values from 0.099609375 to 1.8984375
- gain_key: bfloat16 [16, 2048], P('section'), may hold values from 0.099609375 to 1.8984375
Outputs:
- mixed: bfloat16 [16, 8192, 2048], P('section', 'ctx')
The draws below stay inside these ranges and needn't reach their ends.
Inputs may be any that keep to these rules, and one draw needn't show every extreme that they name: `segments`: along the events of a micro-batch the ids never fall and each of the two ids 0, 1 is used.
All inputs are finite; a program needn't handle non-finite values.
Results may differ from the reference program's by a relative error of at most 0.004.
The reference program's roundings to bfloat16 on the way count: a program that leaves them out, or rounds other values in their place, can miss the bound.
Values may be sent and summed in bfloat16 or wider, within the bound.
No kernel may reach another device: no remote copies, remote signals or barrier semaphores. Data moves between devices by JAX's collectives and lax.ppermute only.
A program may use at most 64 MiB of HBM per device.

```python
import math
import jax
import jax.numpy as jnp
from jax import lax

H = 16
HD = 128
TOK_DEV = 256
HOPS = 3
WINDOW = 768
TOKENS = 8192
SECTIONS = 16


def shared_pair(key):
    base = jax.random.fold_in(key, 4242)
    first_key, second_key = jax.random.split(base, 2)
    shape = (SECTIONS, TOKENS, H * HD)
    query_raw = jnp.clip(jax.random.normal(first_key, shape, jnp.float32), -8.0, 8.0)
    key_raw = jnp.clip(jax.random.normal(second_key, shape, jnp.float32), -8.0, 8.0)
    return (query_raw, key_raw)


def draw_queries(key, part):
    return shared_pair(key)[0].astype(jnp.bfloat16)


def draw_keys(key, part):
    return shared_pair(key)[1].astype(jnp.bfloat16)


def draw_segments(key, part):
    base = jax.random.fold_in(key, 7171)
    cut = jax.random.randint(base, (SECTIONS, 1), TOKENS // 4, 3 * TOKENS // 4)
    position = jnp.arange(TOKENS, dtype=jnp.int32)[None, :]
    return (position >= cut).astype(jnp.int32)


def block_levels(own_key, dims, pieces, least, top_value):
    def one(dim, shards_of):
        heights = jax.random.uniform(jax.random.fold_in(jax.random.fold_in(own_key, 6), dim), (shards_of,), jnp.float32, least / len(pieces), top_value / len(pieces))
        return jnp.repeat(jnp.exp(heights), dims[dim] // shards_of).reshape((-1,) + (1,) * (len(dims) - dim - 1))

    factor_of = one(*pieces[0])
    for cut in pieces[1:]:
        factor_of = factor_of * one(*cut)
    return factor_of


def noise(own_key, extent, width, reach, cuts=(), kind=jnp.bfloat16):
    drawn = width * jax.random.normal(own_key, extent, jnp.float32)
    if cuts:
        drawn = drawn * block_levels(own_key, extent, cuts, -0.22, 0.18)
    return jnp.clip(drawn, -reach, reach).astype(kind)


def setup_inputs(seed: int = 0) -> dict:
    streams_of = jax.random.split(jax.random.key(seed), 7)
    return {
        "queries": draw_queries(jax.random.fold_in(streams_of[6], 71), 0),
        "keys": draw_keys(jax.random.fold_in(streams_of[6], 71), 0),
        "values": noise(streams_of[2], (SECTIONS, TOKENS, H * HD), 1.0, 6.0, ((0, 16), (1, 32))),
        "segments": draw_segments(jax.random.fold_in(streams_of[6], 71), 0),
        "gain_query": jnp.clip(1.0 + 0.18 * jax.random.normal(streams_of[4], (SECTIONS, H * HD), jnp.float32), 0.099609375, 1.8984375).astype(jnp.bfloat16),
        "gain_key": jnp.clip(1.0 + 0.18 * jax.random.normal(streams_of[5], (SECTIONS, H * HD), jnp.float32), 0.099609375, 1.8984375).astype(jnp.bfloat16),
    }


NEG = -1e+30

def attend_all(queries, keys, values, segrow, score_scale):
    token_count = queries.shape[0]
    full_width = queries.shape[1]
    head_count = full_width // HD
    span = (HOPS + 1) * TOK_DEV
    block_count = token_count // TOK_DEV
    padded_keys = jnp.concatenate([jnp.zeros((HOPS * TOK_DEV, full_width), keys.dtype), keys], axis=0)
    padded_values = jnp.concatenate([jnp.zeros((HOPS * TOK_DEV, full_width), values.dtype), values], axis=0)
    padded_seg = jnp.concatenate([jnp.full((HOPS * TOK_DEV,), -1, jnp.int32), segrow.astype(jnp.int32)])

    def one_block(block_index):
        start = (block_index * TOK_DEV).astype(jnp.int32)
        query_b = lax.dynamic_slice_in_dim(queries, start, TOK_DEV, 0).astype(jnp.float32).reshape(TOK_DEV, head_count, HD)
        key_b = lax.dynamic_slice_in_dim(padded_keys, start, span, 0).astype(jnp.float32).reshape(span, head_count, HD)
        value_b = lax.dynamic_slice_in_dim(padded_values, start, span, 0).astype(jnp.float32).reshape(span, head_count, HD)
        query_seg = lax.dynamic_slice_in_dim(segrow.astype(jnp.int32), start, TOK_DEV, 0)
        key_seg = lax.dynamic_slice_in_dim(padded_seg, start, span, 0)
        query_pos = start + jnp.arange(TOK_DEV, dtype=jnp.int32)
        key_pos = start - HOPS * TOK_DEV + jnp.arange(span, dtype=jnp.int32)
        allowed = (query_seg[:, None] == key_seg[None, :]) & (key_pos[None, :] <= query_pos[:, None]) & (key_pos[None, :] > query_pos[:, None] - WINDOW) & (key_seg[None, :] >= 0)
        scores = jnp.einsum('qhd,khd->hqk', query_b, key_b) * score_scale
        scores = jnp.where(allowed[None], scores, NEG)
        row_max = lax.optimization_barrier(jnp.max(scores, axis=2, keepdims=True))
        probs = jnp.where(allowed[None], jnp.exp(scores - row_max), 0.0)
        row_total = lax.optimization_barrier(jnp.sum(probs, axis=2))
        rounded = lax.optimization_barrier(probs.astype(jnp.bfloat16)).astype(jnp.float32)
        result = jnp.einsum('hqk,khd->qhd', rounded, value_b) / jnp.transpose(row_total)[:, :, None]
        return result.reshape(TOK_DEV, full_width).astype(jnp.bfloat16)
    blocks = lax.map(one_block, jnp.arange(block_count, dtype=jnp.int32))
    return blocks.reshape(token_count, full_width)

def normalize(received):
    shaped = received.astype(jnp.float32).reshape(received.shape[0], received.shape[1], -1, HD)
    mean_square = lax.optimization_barrier(jnp.mean(shaped * shaped, axis=3, keepdims=True))
    return (shaped * lax.rsqrt(mean_square + 1e-06)).reshape(received.shape).astype(jnp.bfloat16)

def reference(queries, keys, values, segments, gain_query, gain_key):
    first_scale = 1.0 / math.sqrt(HD)
    second_scale = 1.0 / HD

    def first_layer(items):
        return attend_all(items[0], items[1], items[2], items[3], first_scale)

    def second_layer(items):
        return attend_all(items[0], items[1], items[2], items[3], second_scale)
    first_out = lax.map(first_layer, (queries, keys, values, segments))
    received = jnp.roll(first_out, 1, axis=0)
    prior_seg = jnp.roll(segments, 1, axis=0)
    normed = normalize(received)
    normed_f = normed.astype(jnp.float32)
    query_two = (normed_f * gain_query.astype(jnp.float32)[:, None, :]).astype(jnp.bfloat16)
    key_two = (normed_f * gain_key.astype(jnp.float32)[:, None, :]).astype(jnp.bfloat16)
    second = lax.map(second_layer, (query_two, key_two, normed, prior_seg))
    mixed = (second.astype(jnp.float32) + normed_f).astype(jnp.bfloat16)
    return mixed
```

```python
import functools
import math

import jax
import jax.numpy as jnp
from jax import lax
from jax.experimental import pallas as pl
from jax.experimental.pallas import tpu as pltpu
from jax.sharding import PartitionSpec as P

HD = 128
HOPS = 3
RING = 8
NEG = -1e30
LOG2E = 1.4426950408889634
BF = jnp.bfloat16
F32 = jnp.float32


def attend(query, keys, values, spot, cut, first, scale, masked):
    rows = query.shape[0]
    row = lax.broadcasted_iota(jnp.int32, (rows, rows), 0)
    col = lax.broadcasted_iota(jnp.int32, (rows, rows), 1)
    own = col <= row

    def score(key):
        return lax.dot_general(query, key, (((1,), (1,)), ((), ())), preferred_element_type=F32)

    parts = [score(key) for key in keys]
    if masked:
        pos = spot + lax.broadcasted_iota(jnp.int32, (rows, 1), 0)
        least = jnp.where(pos >= cut, cut, first)
        for j in range(HOPS + 1):
            begin = spot + (j - HOPS) * rows
            parts[j] = jnp.where(col >= least - begin, parts[j], NEG)
    tiles = [jnp.where(own, parts[HOPS], parts[0])] + parts[1:HOPS]
    peak = tiles[0]
    for tile in tiles[1:]:
        peak = jnp.maximum(peak, tile)
    peak = jnp.max(peak, axis=1, keepdims=True)
    factor = scale * LOG2E
    probs = [jnp.exp2((tile - peak) * factor) for tile in tiles]
    total = probs[0]
    for prob in probs[1:]:
        total = total + prob
    total = jnp.sum(total, axis=1, keepdims=True)
    rounded = [prob.astype(BF) for prob in probs]
    none = jnp.zeros_like(rounded[0])
    weights = [jnp.where(own, none, rounded[0])] + rounded[1:] + [jnp.where(own, rounded[0], none)]
    summed = jnp.zeros((rows, HD), F32)
    for weight, value in zip(weights, values):
        summed = summed + jnp.dot(weight, value, preferred_element_type=F32)
    return (summed / total).astype(BF)


def either(info, spot, rows, run):
    cut, first = info[0], info[1]
    low = spot - HOPS * rows
    need = ((cut > low) & (cut < spot + rows)) | (first > low)

    @pl.when(need)
    def _():
        run(True)

    @pl.when(jnp.logical_not(need))
    def _():
        run(False)


def normalize(block):
    wide = block.astype(F32)
    square = jnp.mean(wide * wide, axis=1, keepdims=True)
    return (wide * lax.rsqrt(square + 1e-06)).astype(BF)


def first_free(scale, info, q, kv, out):
    blocks, heads, rows = q.shape[0], q.shape[1], q.shape[2]

    def step(i, _):
        h, b = i // (blocks - HOPS), HOPS + i % (blocks - HOPS)
        spot = b * rows

        def run(masked):
            keys = [kv[b - HOPS + j, h] for j in range(HOPS + 1)]
            values = [kv[b - HOPS + j, heads + h] for j in range(HOPS + 1)]
            got = attend(q[b, h], keys, values, spot, info[0], info[1], scale, masked)
            out[b - HOPS, h] = normalize(got)

        either(info, spot, rows, run)
        return 0

    lax.fori_loop(0, heads * (blocks - HOPS), step, 0)


def gained(block, gain):
    return (block.astype(F32) * gain.astype(F32)).astype(BF)


def finish(second, normed):
    return (second.astype(F32) + normed.astype(F32)).astype(BF)


def middle(scale_one, scale_two, info, q, kv, halo, later, gains, early, out, key_two):
    blocks, heads, rows = q.shape[0], q.shape[1], q.shape[2]

    def step(h, _):
        for b in range(HOPS):
            spot = b * rows

            def run(masked):
                def pick(t):
                    behind = [halo[j, t] for j in range(b, HOPS)]
                    return behind + [kv[j, t] for j in range(b + 1)]

                got = attend(q[b, h], pick(h), pick(heads + h), spot, info[0], info[1], scale_one, masked)
                early[b, h] = normalize(got)

            either(info, spot, rows, run)
            key_two[b, h] = gained(early[b, h], gains[heads + h])
        for b in range(HOPS, blocks):
            key_two[b, h] = gained(later[b - HOPS, h], gains[heads + h])
        return 0

    lax.fori_loop(0, heads, step, 0)

    def second(h, _):
        for b in range(HOPS, blocks):
            spot = b * rows
            take = lambda j: early[j, h] if j < HOPS else later[j - HOPS, h]

            def run(masked):
                normed = take(b)
                keys = [key_two[j, h] for j in range(b - HOPS, b + 1)]
                values = [take(j) for j in range(b - HOPS, b + 1)]
                got = attend(gained(normed, gains[h]), keys, values, spot, info[0], info[1], scale_two, masked)
                out[b - HOPS, h] = finish(got, normed)

            either(info, spot, rows, run)
        return 0

    lax.fori_loop(0, heads, second, 0)


def last(scale, info, early, halo, gains, out, key_two):
    heads, rows = early.shape[1], early.shape[2]

    def step(h, _):
        for j in range(HOPS):
            key_two[j] = gained(halo[j, h], gains[heads + h])
            key_two[HOPS + j] = gained(early[j, h], gains[heads + h])
        for b in range(HOPS):
            spot = b * rows
            take = lambda j: halo[j, h] if j < HOPS else early[j - HOPS, h]

            def run(masked):
                normed = early[b, h]
                keys = [key_two[j] for j in range(b, b + HOPS + 1)]
                values = [take(j) for j in range(b, b + HOPS + 1)]
                got = attend(gained(normed, gains[h]), keys, values, spot, info[0], info[1], scale, masked)
                out[b, h] = finish(got, normed)

            either(info, spot, rows, run)
        return 0

    lax.fori_loop(0, heads, step, 0)


def call(body, out_shape, scratch, operands, pairs):
    whole = pl.BlockSpec(memory_space=pltpu.VMEM)
    cost = pl.CostEstimate(flops=pairs * HD * 4, bytes_accessed=sum(o.size * 2 for o in operands[1:]), transcendentals=pairs)
    return pl.pallas_call(
        body,
        out_shape=out_shape,
        in_specs=[pl.BlockSpec(memory_space=pltpu.SMEM)] + [whole] * (len(operands) - 1),
        out_specs=jax.tree.map(lambda _: whole, out_shape),
        scratch_shapes=scratch,
        cost_estimate=cost,
        compiler_params=pltpu.CompilerParams(vmem_limit_bytes=48 << 20),
    )(*operands)


def per_device(queries, keys, values, segments, gain_query, gain_key):
    section, sections = lax.axis_index("section"), lax.axis_size("section")
    ctx, ctxs = lax.axis_index("ctx"), lax.axis_size("ctx")
    rows, width = queries.shape[1], queries.shape[2]
    heads = width // HD // RING
    rings = [list(range(r * RING, r * RING + RING)) for r in range(ctxs // RING)]

    def exchange(block):
        return lax.all_to_all(block, "ctx", 0, 0, axis_index_groups=rings)

    def from_ring_before(block):
        return lax.ppermute(block, "ctx", [(i, i + RING) for i in range(ctxs - RING)])

    def next_section(block):
        return lax.ppermute(block, "section", [(i, (i + 1) % sections) for i in range(sections)])

    def by_head(block):
        return jnp.transpose(block[0].reshape(rows, RING, heads, HD), (1, 2, 0, 3))

    own_seg = lax.dynamic_index_in_dim(segments, section, 0, keepdims=False)
    start = (ctx // RING) * (RING * rows)
    cut = own_seg.shape[0] - jnp.sum(own_seg)
    info = jnp.stack([cut - start, -start]).astype(jnp.int32)
    gains = jnp.concatenate([gain_query, gain_key], axis=0)
    gains = lax.ppermute(gains, "section", [((i + 1) % sections, i) for i in range(sections)])
    gains = lax.dynamic_slice_in_dim(gains, (ctx % RING) * heads * HD, heads * HD, 1)
    gains = gains.reshape(2 * heads, 1, HD)

    kv = exchange(jnp.concatenate([by_head(keys), by_head(values)], axis=1))
    halo = from_ring_before(kv[RING - HOPS :])
    q = exchange(by_head(queries))

    free = RING - HOPS
    scale_one, scale_two = 1.0 / math.sqrt(HD), 1.0 / HD
    shape = lambda n: jax.ShapeDtypeStruct((n, heads, rows, HD), BF)
    tile_pairs = heads * rows * rows * (HOPS + 1)
    later = call(functools.partial(first_free, scale_one), shape(free), [], (info, q, kv), free * tile_pairs)
    halo_two = from_ring_before(later[free - HOPS :])
    early, done_later = call(
        functools.partial(middle, scale_one, scale_two),
        (shape(HOPS), shape(free)),
        [pltpu.VMEM((RING, heads, rows, HD), BF)],
        (info, q, kv, halo, later, gains),
        RING * tile_pairs,
    )
    sent_later = next_section(done_later)
    done_early = call(
        functools.partial(last, scale_two),
        shape(HOPS),
        [pltpu.VMEM((2 * HOPS, rows, HD), BF)],
        (info, early, halo_two, gains),
        HOPS * tile_pairs,
    )
    sent_early = next_section(done_early)
    mixed = exchange(jnp.concatenate([sent_early, sent_later], axis=0))
    return jnp.transpose(mixed, (2, 0, 1, 3)).reshape(1, rows, width)


def solution(mesh):
    return jax.shard_map(
        per_device,
        mesh=mesh,
        in_specs=(
            P("section", "ctx", None),
            P("section", "ctx", None),
            P("section", "ctx", None),
            P(),
            P("section", None),
            P("section", None),
        ),
        out_specs=P("section", "ctx", None),
        check_vma=False,
    )
```

```python
import functools
import math

import jax
import jax.numpy as jnp
from jax import lax
from jax.experimental import pallas as pl
from jax.experimental.pallas import tpu as pltpu
from jax.sharding import PartitionSpec as P


HD = 128
HOPS = 3
RING = 8
NEG = -1e30
LOG2E = 1.4426950408889634
BF = jnp.bfloat16
F32 = jnp.float32


def attend(query, keys, values, spot, cut, first, scale, masked):
    rows = query.shape[0]
    row = lax.broadcasted_iota(jnp.int32, (rows, rows), 0)
    col = lax.broadcasted_iota(jnp.int32, (rows, rows), 1)
    own = col <= row

    def score(key):
        return lax.dot_general(query, key, (((1,), (1,)), ((), ())), preferred_element_type=F32)

    parts = [score(key) for key in keys]
    if masked:
        pos = spot + lax.broadcasted_iota(jnp.int32, (rows, 1), 0)
        least = jnp.where(pos >= cut, cut, first)
        for j in range(HOPS + 1):
            begin = spot + (j - HOPS) * rows
            parts[j] = jnp.where(col >= least - begin, parts[j], NEG)
    tiles = [jnp.where(own, parts[HOPS], parts[0])] + parts[1:HOPS]
    peak = tiles[0]
    for tile in tiles[1:]:
        peak = jnp.maximum(peak, tile)
    peak = jnp.max(peak, axis=1, keepdims=True)
    factor = scale * LOG2E
    probs = [jnp.exp2((tile - peak) * factor) for tile in tiles]
    total = probs[0]
    for prob in probs[1:]:
        total = total + prob
    total = jnp.sum(total, axis=1, keepdims=True)
    rounded = [prob.astype(BF) for prob in probs]
    none = jnp.zeros_like(rounded[0])
    weights = [jnp.where(own, none, rounded[0])] + rounded[1:] + [jnp.where(own, rounded[0], none)]
    summed = jnp.zeros((rows, HD), F32)
    for weight, value in zip(weights, values):
        summed = summed + jnp.dot(weight, value, preferred_element_type=F32)
    return (summed / total).astype(BF)


def either(info, spot, rows, run):
    cut, first = info[0], info[1]
    low = spot - HOPS * rows
    need = ((cut > low) & (cut < spot + rows)) | (first > low)

    @pl.when(need)
    def _():
        run(True)

    @pl.when(jnp.logical_not(need))
    def _():
        run(False)


def normalize(block):
    wide = block.astype(F32)
    square = jnp.mean(wide * wide, axis=1, keepdims=True)
    return (wide * lax.rsqrt(square + 1e-06)).astype(BF)


def rows_of(ref):
    return ref.shape[-2]


def first_free(h, scale, info, q, kv, out, tail):
    blocks, rows = kv.shape[0], rows_of(kv)

    def step(b, _):
        spot = b * rows

        def run(masked):
            keys = [kv[b - HOPS + j, 0] for j in range(HOPS + 1)]
            values = [kv[b - HOPS + j, 1] for j in range(HOPS + 1)]
            got = attend(q[b, h], keys, values, spot, info[0], info[1], scale, masked)
            out[b - HOPS] = normalize(got)

        either(info, spot, rows, run)
        return 0

    lax.fori_loop(HOPS, blocks, step, 0)
    for j in range(HOPS):
        tail[j] = out[out.shape[0] - HOPS + j]


def gained(block, gain):
    return (block.astype(F32) * gain.astype(F32)).astype(BF)


def finish(second, normed):
    return (second.astype(F32) + normed.astype(F32)).astype(BF)


def middle(h, heads, scale_one, scale_two, info, q, kv, halo, later, gains, early, out, normed, key_two):
    blocks, rows = kv.shape[0], rows_of(kv)
    for b in range(HOPS):
        spot = b * rows

        def run(masked):
            def pick(t):
                return [halo[j, t] for j in range(b, HOPS)] + [kv[j, t] for j in range(b + 1)]

            got = attend(q[b, h], pick(0), pick(1), spot, info[0], info[1], scale_one, masked)
            early[b] = normalize(got)

        either(info, spot, rows, run)
    for b in range(blocks):
        block = early[b] if b < HOPS else later[b - HOPS]
        normed[b] = block
        key_two[b] = gained(block, gains[heads + h])

    def second(b, _):
        spot = b * rows

        def run(masked):
            keys = [key_two[b - HOPS + j] for j in range(HOPS + 1)]
            values = [normed[b - HOPS + j] for j in range(HOPS + 1)]
            got = attend(gained(normed[b], gains[h]), keys, values, spot, info[0], info[1], scale_two, masked)
            out[b - HOPS] = finish(got, normed[b])

        either(info, spot, rows, run)
        return 0

    lax.fori_loop(HOPS, blocks, second, 0)


def last(h, heads, scale, info, early, later, halo, gains, out, normed, key_two):
    rows = rows_of(early)
    for j in range(HOPS):
        normed[j] = halo[j]
        normed[HOPS + j] = early[j]
    for j in range(2 * HOPS):
        key_two[j] = gained(normed[j], gains[heads + h])

    def step(b, _):
        spot = b * rows

        def run(masked):
            mine = normed[b + HOPS]
            keys = [key_two[b + j] for j in range(HOPS + 1)]
            values = [normed[b + j] for j in range(HOPS + 1)]
            got = attend(gained(mine, gains[h]), keys, values, spot, info[0], info[1], scale, masked)
            out[b] = finish(got, mine)

        either(info, spot, rows, run)
        return 0

    lax.fori_loop(0, HOPS, step, 0)
    for j in range(later.shape[0]):
        out[HOPS + j] = later[j]


CUTS = 4


def pack(where, keys, values, queries, segments, *rest):
    heads = (len(rest) - 8) // 2
    outs, q_out, info = rest[:heads], rest[heads], rest[heads + 1]
    staged, q_staged = rest[heads + 2 : 2 * heads + 2], rest[2 * heads + 2]
    held, ids, in_sem, id_sem, out_sem = rest[2 * heads + 3 :]
    rows = keys.shape[0] // CUTS
    sources = (keys, values, queries)

    def load(t, c):
        part = pl.ds(c * rows, rows)
        return pltpu.make_async_copy(sources[t].at[part], held.at[t, part], in_sem.at[t, c])

    def store(h, r):
        source, target = (staged[h], outs[h]) if h < heads else (q_staged, q_out)
        return pltpu.make_async_copy(source.at[r], target.at[r], out_sem.at[h, r])

    wide = pltpu.make_async_copy(segments, ids, id_sem)
    for t in range(3):
        for c in range(CUTS):
            load(t, c).start()
    wide.start()
    for t in range(2):
        for c in range(CUTS):
            load(t, c).wait()
    for h in range(heads):
        for r in range(RING):
            at = (r * heads + h) * HD
            for t in range(2):
                staged[h][r, t] = held[t, :, at : at + HD]
            store(h, r).start()
    for c in range(CUTS):
        load(2, c).wait()
    for r in range(RING):
        for h in range(heads):
            at = (r * heads + h) * HD
            q_staged[r, h] = held[2, :, at : at + HD]
        store(heads, r).start()
    wide.wait()
    ones = jnp.sum(ids[pl.ds(where[0], 1), :])
    info[0] = ids.shape[1] - ones - where[1]
    info[1] = -where[1]
    for h in range(heads + 1):
        for r in range(RING):
            store(h, r).wait()


def packed(where, keys, values, queries, segments, heads):
    rows, width = keys.shape
    block = (RING, 2, rows, HD)
    blocks = [block] * heads + [(RING, heads, rows, HD)]
    anywhere = pl.BlockSpec(memory_space=pl.ANY)
    return pl.pallas_call(
        pack,
        out_shape=[jax.ShapeDtypeStruct(dims, BF) for dims in blocks] + [jax.ShapeDtypeStruct((2,), jnp.int32)],
        in_specs=[pl.BlockSpec(memory_space=pltpu.SMEM)] + [anywhere] * 4,
        out_specs=[anywhere] * (heads + 1) + [pl.BlockSpec(memory_space=pltpu.SMEM)],
        scratch_shapes=[pltpu.VMEM(dims, BF) for dims in blocks]
        + [
            pltpu.VMEM((3, rows, width), BF),
            pltpu.VMEM(segments.shape, jnp.int32),
            pltpu.SemaphoreType.DMA((3, CUTS)),
            pltpu.SemaphoreType.DMA,
            pltpu.SemaphoreType.DMA((heads + 1, RING)),
        ],
        cost_estimate=pl.CostEstimate(flops=0, bytes_accessed=3 * rows * width * 4, transcendentals=0),
        name="pack",
    )(where, keys, values, queries, segments)


def unpack(*refs):
    ins, out = refs[:-1], refs[-1]
    for h, block in enumerate(ins):
        for r in range(RING):
            at = (r * len(ins) + h) * HD
            out[:, at : at + HD] = block[r]


def call(body, out_shape, operands, pairs=0, scalars=0, scratch=()):
    return call_kernel(body, out_shape, operands, pairs, scalars, scratch)


def call_kernel(body, out_shape, operands, pairs, scalars, scratch):
    whole = pl.BlockSpec(memory_space=pltpu.VMEM)
    outs = jax.tree.leaves(out_shape)
    moved = sum(o.size * 2 for o in [*operands[scalars:], *outs])
    return pl.pallas_call(
        body,
        out_shape=out_shape,
        in_specs=[pl.BlockSpec(memory_space=pltpu.SMEM)] * scalars + [whole] * (len(operands) - scalars),
        out_specs=jax.tree.map(lambda _: whole, out_shape),
        scratch_shapes=list(scratch),
        cost_estimate=pl.CostEstimate(flops=pairs * HD * 4, bytes_accessed=moved, transcendentals=pairs),
        compiler_params=pltpu.CompilerParams(vmem_limit_bytes=40 << 20),
    )(*operands)


def program(queries, keys, values, segments, gain_query, gain_key):
    section, sections = lax.axis_index("section"), lax.axis_size("section")
    ctx, ctxs = lax.axis_index("ctx"), lax.axis_size("ctx")
    rows, width = queries.shape[1], queries.shape[2]
    heads = width // HD // RING
    rings = [list(range(r * RING, r * RING + RING)) for r in range(ctxs // RING)]

    def exchange(block):
        return lax.all_to_all(block, "ctx", 0, 0, axis_index_groups=rings)

    def from_ring_before(block):
        return lax.ppermute(block, "ctx", [(i, i + RING) for i in range(ctxs - RING)])

    def next_section(block):
        return lax.ppermute(block, "section", [(i, (i + 1) % sections) for i in range(sections)])

    def shape(*dims):
        return jax.ShapeDtypeStruct((*dims, rows, HD), BF)

    where = jnp.stack([section, (ctx // RING) * (RING * rows)]).astype(jnp.int32)
    *ready, ready_q, info = packed(where, keys[0], values[0], queries[0], segments, heads)
    gains = jnp.concatenate([gain_query, gain_key], axis=0)
    gains = lax.ppermute(gains, "section", [((i + 1) % sections, i) for i in range(sections)])
    gains = lax.dynamic_slice_in_dim(gains, (ctx % RING) * heads * HD, heads * HD, 1)
    gains = gains.reshape(2 * heads, 1, HD)

    kvs, halos = [], []
    for h in range(heads):
        kv = exchange(ready[h])
        kvs.append(kv)
        halos.append(from_ring_before(kv[RING - HOPS :]))

    q = exchange(ready_q)

    free = RING - HOPS
    scale_one, scale_two = 1.0 / math.sqrt(HD), 1.0 / HD
    tile_pairs = rows * rows * (HOPS + 1)
    done = []
    for h in range(heads):
        later, tail = call(
            functools.partial(first_free, h, scale_one), (shape(free), shape(HOPS)), (info, q, kvs[h]), free * tile_pairs, 1
        )
        halo_two = from_ring_before(tail)
        early, done_later = call(
            functools.partial(middle, h, heads, scale_one, scale_two),
            (shape(HOPS), shape(free)),
            (info, q, kvs[h], halos[h], later, gains),
            RING * tile_pairs,
            1,
            [pltpu.VMEM((RING, rows, HD), BF)] * 2,
        )
        whole = call(
            functools.partial(last, h, heads, scale_two),
            shape(RING),
            (info, early, done_later, halo_two, gains),
            HOPS * tile_pairs,
            1,
            [pltpu.VMEM((2 * HOPS, rows, HD), BF)] * 2,
        )
        done.append(next_section(exchange(whole)))
    return call(unpack, jax.ShapeDtypeStruct((rows, width), BF), tuple(done))[None]


def solution(mesh):
    return jax.shard_map(
        program,
        mesh=mesh,
        in_specs=(
            P("section", "ctx", None),
            P("section", "ctx", None),
            P("section", "ctx", None),
            P(),
            P("section", None),
            P("section", None),
        ),
        out_specs=P("section", "ctx", None),
        check_vma=False,
    )
```

```python
import functools
import math

import jax
import jax.numpy as jnp
from jax import lax
from jax.experimental import pallas as pl
from jax.experimental.pallas import tpu as pltpu
from jax.sharding import PartitionSpec as P


HD = 128
HOPS = 3
RING = 8
NEG = -1e30
LOG2E = 1.4426950408889634
BF = jnp.bfloat16
F32 = jnp.float32


def attend(query, keys, values, spot, cut, first, scale, masked):
    rows = query.shape[0]
    row = lax.broadcasted_iota(jnp.int32, (rows, rows), 0)
    col = lax.broadcasted_iota(jnp.int32, (rows, rows), 1)
    own = col <= row

    def score(key):
        return lax.dot_general(query, key, (((1,), (1,)), ((), ())), preferred_element_type=F32)

    parts = [score(key) for key in keys]
    if masked:
        pos = spot + lax.broadcasted_iota(jnp.int32, (rows, 1), 0)
        least = jnp.where(pos >= cut, cut, first)
        for j in range(HOPS + 1):
            begin = spot + (j - HOPS) * rows
            parts[j] = jnp.where(col >= least - begin, parts[j], NEG)
    tiles = [jnp.where(own, parts[HOPS], parts[0])] + parts[1:HOPS]
    peak = tiles[0]
    for tile in tiles[1:]:
        peak = jnp.maximum(peak, tile)
    peak = jnp.max(peak, axis=1, keepdims=True)
    factor = scale * LOG2E
    probs = [jnp.exp2((tile - peak) * factor) for tile in tiles]
    total = probs[0]
    for prob in probs[1:]:
        total = total + prob
    total = jnp.sum(total, axis=1, keepdims=True)
    rounded = [prob.astype(BF) for prob in probs]
    none = jnp.zeros_like(rounded[0])
    weights = [jnp.where(own, none, rounded[0])] + rounded[1:] + [jnp.where(own, rounded[0], none)]
    summed = jnp.zeros((rows, HD), F32)
    for weight, value in zip(weights, values):
        summed = summed + jnp.dot(weight, value, preferred_element_type=F32)
    return (summed / total).astype(BF)


def either(info, spot, rows, run):
    cut, first = info[0], info[1]
    low = spot - HOPS * rows
    need = ((cut > low) & (cut < spot + rows)) | (first > low)

    @pl.when(need)
    def _():
        run(True)

    @pl.when(jnp.logical_not(need))
    def _():
        run(False)


def normalize(block):
    wide = block.astype(F32)
    square = jnp.mean(wide * wide, axis=1, keepdims=True)
    return (wide * lax.rsqrt(square + 1e-06)).astype(BF)


def rows_of(ref):
    return ref.shape[-2]


def first_free(scale, info, kv, out, tail):
    blocks, rows = kv.shape[0], rows_of(kv)

    def step(b, _):
        spot = b * rows

        def run(masked):
            keys = [kv[b - HOPS + j, 0] for j in range(HOPS + 1)]
            values = [kv[b - HOPS + j, 1] for j in range(HOPS + 1)]
            got = attend(kv[b, 2], keys, values, spot, info[0], info[1], scale, masked)
            out[b - HOPS] = normalize(got)

        either(info, spot, rows, run)
        return 0

    lax.fori_loop(HOPS, blocks, step, 0)
    for j in range(HOPS):
        tail[j] = out[out.shape[0] - HOPS + j]


def gained(block, gain):
    return (block.astype(F32) * gain.astype(F32)).astype(BF)


def finish(second, normed):
    return (second.astype(F32) + normed.astype(F32)).astype(BF)


def middle(scale_one, scale_two, info, kv, halo, later, gains, early, out, normed, key_two):
    blocks, rows = kv.shape[0], rows_of(kv)
    for b in range(HOPS):
        spot = b * rows

        def run(masked):
            def pick(t):
                return [halo[j, t] for j in range(b, HOPS)] + [kv[j, t] for j in range(b + 1)]

            got = attend(kv[b, 2], pick(0), pick(1), spot, info[0], info[1], scale_one, masked)
            early[b] = normalize(got)

        either(info, spot, rows, run)
    for b in range(blocks):
        block = early[b] if b < HOPS else later[b - HOPS]
        normed[b] = block
        key_two[b] = gained(block, gains[1])

    def second(b, _):
        spot = b * rows

        def run(masked):
            keys = [key_two[b - HOPS + j] for j in range(HOPS + 1)]
            values = [normed[b - HOPS + j] for j in range(HOPS + 1)]
            got = attend(gained(normed[b], gains[0]), keys, values, spot, info[0], info[1], scale_two, masked)
            out[b - HOPS] = finish(got, normed[b])

        either(info, spot, rows, run)
        return 0

    lax.fori_loop(HOPS, blocks, second, 0)


def last(scale, info, early, later, halo, gains, out, normed, key_two):
    rows = rows_of(early)
    for j in range(HOPS):
        normed[j] = halo[j]
        normed[HOPS + j] = early[j]
    for j in range(2 * HOPS):
        key_two[j] = gained(normed[j], gains[1])

    def step(b, _):
        spot = b * rows

        def run(masked):
            mine = normed[b + HOPS]
            keys = [key_two[b + j] for j in range(HOPS + 1)]
            values = [normed[b + j] for j in range(HOPS + 1)]
            got = attend(gained(mine, gains[0]), keys, values, spot, info[0], info[1], scale, masked)
            out[b] = finish(got, mine)

        either(info, spot, rows, run)
        return 0

    lax.fori_loop(0, HOPS, step, 0)
    for j in range(later.shape[0]):
        out[HOPS + j] = later[j]


CUTS = 4


def pack(where, keys, values, queries, segments, *rest):
    heads = (len(rest) - 7) // 2
    outs, infos, staged = rest[:heads], rest[heads : heads + 2], rest[heads + 2 : 2 * heads + 2]
    held, ids, in_sem, id_sem, out_sem = rest[2 * heads + 2 :]
    rows = keys.shape[0] // CUTS
    wide = pltpu.make_async_copy(segments, ids, id_sem)
    ins = []
    for t, ref in enumerate((keys, values, queries)):
        for c in range(CUTS):
            part = pl.ds(c * rows, rows)
            ins.append(pltpu.make_async_copy(ref.at[part], held.at[t, part], in_sem.at[t, c]))
            ins[-1].start()
    wide.start()
    for copy in ins:
        copy.wait()
    sends = []
    for h in reversed(range(heads)):
        for r in range(RING):
            at = (r * heads + h) * HD
            for t in range(3):
                staged[h][r, t] = held[t, :, at : at + HD]
        for r in range(RING):
            sends.append(pltpu.make_async_copy(staged[h].at[r], outs[h].at[r], out_sem.at[h, r]))
            sends[-1].start()
    wide.wait()
    for i, info in enumerate(infos):
        ones = jnp.sum(ids[pl.ds(where[i], 1), :])
        info[0] = ids.shape[1] - ones - where[2]
        info[1] = -where[2]
    for copy in sends:
        copy.wait()


def packed(where, keys, values, queries, segments, heads):
    rows, width = keys.shape
    block = (RING, 3, rows, HD)
    anywhere = pl.BlockSpec(memory_space=pl.ANY)
    return pl.pallas_call(
        pack,
        out_shape=[jax.ShapeDtypeStruct(block, BF)] * heads + [jax.ShapeDtypeStruct((2,), jnp.int32)] * 2,
        in_specs=[pl.BlockSpec(memory_space=pltpu.SMEM)] + [anywhere] * 4,
        out_specs=[anywhere] * heads + [pl.BlockSpec(memory_space=pltpu.SMEM)] * 2,
        scratch_shapes=[pltpu.VMEM(block, BF)] * heads
        + [
            pltpu.VMEM((3, rows, width), BF),
            pltpu.VMEM(segments.shape, jnp.int32),
            pltpu.SemaphoreType.DMA((3, CUTS)),
            pltpu.SemaphoreType.DMA,
            pltpu.SemaphoreType.DMA((heads, RING)),
        ],
        cost_estimate=pl.CostEstimate(flops=0, bytes_accessed=3 * rows * width * 4, transcendentals=0),
        name="pack",
    )(where, keys, values, queries, segments)


def unpack(*refs):
    ins, out = refs[:-1], refs[-1]
    for h, block in enumerate(ins):
        for r in range(RING):
            at = (r * len(ins) + h) * HD
            out[:, at : at + HD] = block[r]


def call(body, out_shape, operands, pairs=0, scalars=0, scratch=()):
    return call_kernel(body, out_shape, operands, pairs, scalars, scratch)


def call_kernel(body, out_shape, operands, pairs, scalars, scratch):
    whole = pl.BlockSpec(memory_space=pltpu.VMEM)
    outs = jax.tree.leaves(out_shape)
    moved = sum(o.size * 2 for o in [*operands[scalars:], *outs])
    return pl.pallas_call(
        body,
        out_shape=out_shape,
        in_specs=[pl.BlockSpec(memory_space=pltpu.SMEM)] * scalars + [whole] * (len(operands) - scalars),
        out_specs=jax.tree.map(lambda _: whole, out_shape),
        scratch_shapes=list(scratch),
        cost_estimate=pl.CostEstimate(flops=pairs * HD * 4, bytes_accessed=moved, transcendentals=pairs),
        compiler_params=pltpu.CompilerParams(vmem_limit_bytes=40 << 20),
    )(*operands)


def program(queries, keys, values, segments, gain_query, gain_key):
    section, sections = lax.axis_index("section"), lax.axis_size("section")
    ctx, ctxs = lax.axis_index("ctx"), lax.axis_size("ctx")
    rows, width = queries.shape[1], queries.shape[2]
    heads = width // HD // RING
    rings = [list(range(r * RING, r * RING + RING)) for r in range(ctxs // RING)]

    def exchange(block):
        return lax.all_to_all(block, "ctx", 0, 0, axis_index_groups=rings)

    def from_ring_before(block):
        return lax.ppermute(block, "ctx", [(i, i + RING) for i in range(ctxs - RING)])

    def next_section(block):
        return lax.ppermute(block, "section", [(i, (i + 1) % sections) for i in range(sections)])

    def shape(*dims):
        return jax.ShapeDtypeStruct((*dims, rows, HD), BF)

    prior = (section + sections - 1) % sections
    where = jnp.stack([section, prior, (ctx // RING) * (RING * rows)]).astype(jnp.int32)
    *ready, own_info, prior_info = packed(where, keys[0], values[0], queries[0], segments, heads)
    moves_first = [h == heads - 1 for h in range(heads)]
    own_gains = jnp.concatenate([gain_query, gain_key], axis=0)
    next_gains = lax.ppermute(own_gains, "section", [((i + 1) % sections, i) for i in range(sections)])

    def of_head(gains, h):
        return lax.dynamic_slice_in_dim(gains, ((ctx % RING) * heads + h) * HD, HD, 1).reshape(2, 1, HD)

    gains = [of_head(own_gains if moves_first[h] else next_gains, h) for h in range(heads)]
    infos = [prior_info if moves_first[h] else own_info for h in range(heads)]
    ready = [next_section(ready[h]) if moves_first[h] else ready[h] for h in range(heads)]

    kvs, halos = [], []
    for h in range(heads):
        kv = exchange(ready[h])
        kvs.append(kv)
        halos.append(from_ring_before(kv[RING - HOPS :, :2]))

    free = RING - HOPS
    scale_one, scale_two = 1.0 / math.sqrt(HD), 1.0 / HD
    tile_pairs = rows * rows * (HOPS + 1)
    done = []
    for h in range(heads):
        later, tail = call(
            functools.partial(first_free, scale_one), (shape(free), shape(HOPS)), (infos[h], kvs[h]), free * tile_pairs, 1
        )
        halo_two = from_ring_before(tail)
        early, done_later = call(
            functools.partial(middle, scale_one, scale_two),
            (shape(HOPS), shape(free)),
            (infos[h], kvs[h], halos[h], later, gains[h]),
            RING * tile_pairs,
            1,
            [pltpu.VMEM((RING, rows, HD), BF)] * 2,
        )
        whole = call(
            functools.partial(last, scale_two),
            shape(RING),
            (infos[h], early, done_later, halo_two, gains[h]),
            HOPS * tile_pairs,
            1,
            [pltpu.VMEM((2 * HOPS, rows, HD), BF)] * 2,
        )
        whole = exchange(whole)
        done.append(whole if moves_first[h] else next_section(whole))
    return call(unpack, jax.ShapeDtypeStruct((rows, width), BF), tuple(done))[None]


def solution(mesh):
    return jax.shard_map(
        program,
        mesh=mesh,
        in_specs=(
            P("section", "ctx", None),
            P("section", "ctx", None),
            P("section", "ctx", None),
            P(),
            P("section", None),
            P("section", None),
        ),
        out_specs=P("section", "ctx", None),
        check_vma=False,
    )
```

```python
import functools
import math

import jax
import jax.numpy as jnp
from jax import lax
from jax.experimental import pallas as pl
from jax.experimental.pallas import tpu as pltpu
from jax.sharding import PartitionSpec as P


HD = 128
HOPS = 3
RING = 8
NEG = -1e30
LOG2E = 1.4426950408889634
BF = jnp.bfloat16
F32 = jnp.float32


def attend(query, keys, values, spot, cut, first, scale, masked):
    parts = [attend_half(query, keys, values, spot, cut, first, scale, masked, low) for low in (0, query.shape[0] // 2)]
    return jnp.concatenate(parts, axis=0)


def attend_half(query, keys, values, spot, cut, first, scale, masked, low):
    rows = query.shape[0]
    half = rows // 2
    col = lax.broadcasted_iota(jnp.int32, (half, half), 1)
    own = col <= lax.broadcasted_iota(jnp.int32, (half, half), 0)
    pos = spot + low + lax.broadcasted_iota(jnp.int32, (half, 1), 0)
    least = jnp.where(pos >= cut, cut, first)

    def score(key, begin):
        got = lax.dot_general(
            query[low : low + half], key, (((1,), (1,)), ((), ())), preferred_element_type=F32
        )
        if masked:
            place = begin + lax.broadcasted_iota(jnp.int32, got.shape, 1)
            got = jnp.where(place >= least, got, NEG)
        return got

    back = spot - HOPS * rows
    if low:
        behind, mine = score(keys[0][half:], back + half), score(keys[HOPS], spot)
        behind_tile, mixed, mine_tile = None, jnp.where(own, mine[:, half:], behind), mine[:, :half]
    else:
        behind, mine = score(keys[0], back), score(keys[HOPS][:half], spot)
        behind_tile, mixed, mine_tile = behind[:, half:], jnp.where(own, mine, behind[:, :half]), None
    single = mine_tile if low else behind_tile
    tiles = [mixed, single] + [score(keys[j], back + j * rows) for j in range(1, HOPS)]
    narrow = [tiles[0], tiles[1]]
    for tile in tiles[2:]:
        narrow += [tile[:, :half], tile[:, half:]]
    peak = functools.reduce(jnp.maximum, narrow)
    peak = jnp.max(peak, axis=1, keepdims=True)
    factor = scale * LOG2E
    probs = [jnp.exp2((tile - peak) * factor) for tile in tiles]
    narrow = [probs[0], probs[1]]
    for prob in probs[2:]:
        narrow += [prob[:, :half], prob[:, half:]]
    total = jnp.sum(functools.reduce(jnp.add, narrow), axis=1, keepdims=True)
    mixed_own = jnp.where(own, probs[0], 0.0).astype(BF)
    mixed_behind = jnp.where(own, 0.0, probs[0]).astype(BF)
    alone = probs[1].astype(BF)

    def times(weight, value):
        return jnp.dot(weight, value, preferred_element_type=F32)

    if low:
        summed = times(mixed_behind, values[0][half:])
        last = times(jnp.concatenate([alone, mixed_own], axis=1), values[HOPS])
    else:
        summed = times(jnp.concatenate([mixed_behind, alone], axis=1), values[0])
        last = times(mixed_own, values[HOPS][:half])
    for j in range(1, HOPS):
        summed = summed + times(probs[1 + j].astype(BF), values[j])
    return ((summed + last) / total).astype(BF)


def either(info, spot, rows, run):
    cut, first = info[0], info[1]
    low = spot - HOPS * rows
    need = ((cut > low) & (cut < spot + rows)) | (first > low)

    @pl.when(need)
    def _():
        run(True)

    @pl.when(jnp.logical_not(need))
    def _():
        run(False)


def normalize(block):
    wide = block.astype(F32)
    square = jnp.mean(wide * wide, axis=1, keepdims=True)
    return (wide * lax.rsqrt(square + 1e-06)).astype(BF)


def rows_of(ref):
    return ref.shape[-2]


def first_free(scale, info, kv, out, tail):
    blocks, rows = kv.shape[0], rows_of(kv)

    def step(b, _):
        spot = b * rows

        def run(masked):
            keys = [kv[b - HOPS + j, 0] for j in range(HOPS + 1)]
            values = [kv[b - HOPS + j, 1] for j in range(HOPS + 1)]
            got = attend(kv[b, 2], keys, values, spot, info[0], info[1], scale, masked)
            out[b - HOPS] = normalize(got)

        either(info, spot, rows, run)
        return 0

    lax.fori_loop(HOPS, blocks, step, 0)
    for j in range(HOPS):
        tail[j] = out[out.shape[0] - HOPS + j]


def gained(block, gain):
    return (block.astype(F32) * gain.astype(F32)).astype(BF)


def finish(second, normed):
    return (second.astype(F32) + normed.astype(F32)).astype(BF)


def second_layer(b, scale, info, normed, key_two, gains, write):
    rows = rows_of(normed)
    spot = b * rows

    def run(masked):
        keys = [key_two[b - HOPS + j] for j in range(HOPS + 1)]
        values = [normed[b - HOPS + j] for j in range(HOPS + 1)]
        got = attend(gained(normed[b], gains[0]), keys, values, spot, info[0], info[1], scale, masked)
        write(finish(got, normed[b]))

    either(info, spot, rows, run)


def ahead(scale, info, later, gains, out, normed, key_two):
    count = later.shape[0]
    for b in range(count):
        normed[HOPS + b] = later[b]
        key_two[HOPS + b] = gained(later[b], gains[1])

    def step(b, _):
        def write(block):
            out[b - 2 * HOPS] = block

        second_layer(b, scale, info, normed, key_two, gains, write)
        return 0

    lax.fori_loop(2 * HOPS, HOPS + count, step, 0)


def middle(scale_one, scale_two, info, kv, halo, later, gains, *rest):
    *known, early, out, normed, key_two = rest
    blocks, rows = kv.shape[0], rows_of(kv)
    stop = 2 * HOPS if known else blocks
    for b in range(HOPS):
        spot = b * rows

        def run(masked):
            def pick(t):
                return [halo[j, t] for j in range(b, HOPS)] + [kv[j, t] for j in range(b + 1)]

            got = attend(kv[b, 2], pick(0), pick(1), spot, info[0], info[1], scale_one, masked)
            early[b] = normalize(got)

        either(info, spot, rows, run)
    for b in range(stop):
        block = early[b] if b < HOPS else later[b - HOPS]
        normed[b] = block
        key_two[b] = gained(block, gains[1])

    def step(b, _):
        def write(block):
            out[b - HOPS] = block

        second_layer(b, scale_two, info, normed, key_two, gains, write)
        return 0

    lax.fori_loop(HOPS, stop, step, 0)
    for b in range(stop, blocks):
        out[b - HOPS] = known[0][b - stop]


def last(scale, info, early, halo, gains, *rest):
    *later, out, normed, key_two = rest
    last_blocks(scale, info, early, later, halo, gains, out, normed, key_two)


def last_blocks(scale, info, early, later, halo, gains, out, normed, key_two):
    rows = rows_of(early)
    for j in range(HOPS):
        normed[j] = halo[j]
        normed[HOPS + j] = early[j]
    for j in range(2 * HOPS):
        key_two[j] = gained(normed[j], gains[1])

    def step(b, _):
        spot = b * rows

        def run(masked):
            mine = normed[b + HOPS]
            keys = [key_two[b + j] for j in range(HOPS + 1)]
            values = [normed[b + j] for j in range(HOPS + 1)]
            got = attend(gained(mine, gains[0]), keys, values, spot, info[0], info[1], scale, masked)
            out[b] = finish(got, mine)

        either(info, spot, rows, run)
        return 0

    lax.fori_loop(0, HOPS, step, 0)
    for known in later:
        for j in range(known.shape[0]):
            out[HOPS + j] = known[j]


def pack(h, heads, keys, values, queries, out, held, in_sem, out_sem):
    def load(r, t):
        source = (keys, values, queries)[t]
        at = pl.ds((r * heads + h) * HD, HD)
        return pltpu.make_async_copy(source.at[:, at], held.at[r, t], in_sem.at[r, t])

    def store(r):
        return pltpu.make_async_copy(held.at[r], out.at[r], out_sem.at[r])

    for r in range(RING):
        for t in range(3):
            load(r, t).start()
    for r in range(RING):
        for t in range(3):
            load(r, t).wait()
        store(r).start()
    for r in range(RING):
        store(r).wait()


def packed(h, heads, keys, values, queries):
    rows = keys.shape[0]
    block = (RING, 3, rows, HD)
    anywhere = pl.BlockSpec(memory_space=pl.ANY)
    return pl.pallas_call(
        functools.partial(pack, h, heads),
        out_shape=jax.ShapeDtypeStruct(block, BF),
        in_specs=[anywhere] * 3,
        out_specs=anywhere,
        scratch_shapes=[pltpu.VMEM(block, BF), pltpu.SemaphoreType.DMA((RING, 3)), pltpu.SemaphoreType.DMA((RING,))],
        cost_estimate=pl.CostEstimate(flops=0, bytes_accessed=RING * 3 * rows * HD * 4, transcendentals=0),
    )(keys, values, queries)


def place(where, segments, info):
    ones = jnp.sum(segments[pl.ds(where[0], 1), :])
    info[0] = segments.shape[1] - ones - where[1]
    info[1] = -where[1]


def placed(where, segments):
    return pl.pallas_call(
        place,
        out_shape=jax.ShapeDtypeStruct((2,), jnp.int32),
        in_specs=[pl.BlockSpec(memory_space=pltpu.SMEM), pl.BlockSpec(memory_space=pltpu.VMEM)],
        out_specs=pl.BlockSpec(memory_space=pltpu.SMEM),
        cost_estimate=pl.CostEstimate(flops=0, bytes_accessed=segments.size * 4, transcendentals=0),
        name="place",
    )(where, segments)


def unpack(*refs):
    ins, out = refs[:-1], refs[-1]
    for h, block in enumerate(ins):
        for r in range(RING):
            at = (r * len(ins) + h) * HD
            out[:, at : at + HD] = block[r]


def call(body, out_shape, operands, pairs=0, scalars=0, scratch=()):
    return call_kernel(body, out_shape, operands, pairs, scalars, scratch)


def call_kernel(body, out_shape, operands, pairs, scalars, scratch):
    whole = pl.BlockSpec(memory_space=pltpu.VMEM)
    outs = jax.tree.leaves(out_shape)
    moved = sum(o.size * 2 for o in [*operands[scalars:], *outs])
    return pl.pallas_call(
        body,
        out_shape=out_shape,
        in_specs=[pl.BlockSpec(memory_space=pltpu.SMEM)] * scalars + [whole] * (len(operands) - scalars),
        out_specs=jax.tree.map(lambda _: whole, out_shape),
        scratch_shapes=list(scratch),
        cost_estimate=pl.CostEstimate(flops=pairs * HD * 4, bytes_accessed=moved, transcendentals=pairs),
        compiler_params=pltpu.CompilerParams(vmem_limit_bytes=40 << 20),
    )(*operands)


def program(queries, keys, values, segments, gain_query, gain_key):
    section, sections = lax.axis_index("section"), lax.axis_size("section")
    ctx, ctxs = lax.axis_index("ctx"), lax.axis_size("ctx")
    rows, width = queries.shape[1], queries.shape[2]
    heads = width // HD // RING
    rings = [list(range(r * RING, r * RING + RING)) for r in range(ctxs // RING)]

    def exchange(block):
        return lax.all_to_all(block, "ctx", 0, 0, axis_index_groups=rings)

    def from_ring_before(block):
        return lax.ppermute(block, "ctx", [(i, i + RING) for i in range(ctxs - RING)])

    def next_section(block):
        return lax.ppermute(block, "section", [(i, (i + 1) % sections) for i in range(sections)])

    def shape(*dims):
        return jax.ShapeDtypeStruct((*dims, rows, HD), BF)

    where = jnp.stack([section, (ctx // RING) * (RING * rows)]).astype(jnp.int32)
    ready = [packed(h, heads, keys[0], values[0], queries[0]) for h in range(heads)]
    info = placed(where, segments)
    gains = jnp.concatenate([gain_query, gain_key], axis=0)
    gains = lax.ppermute(gains, "section", [((i + 1) % sections, i) for i in range(sections)])
    gains = lax.dynamic_slice_in_dim(gains, (ctx % RING) * heads * HD, heads * HD, 1).reshape(2, heads, 1, HD)

    kvs, halos = [], []
    for h in range(heads):
        kv = exchange(ready[h])
        kvs.append(kv)
        halos.append(from_ring_before(kv[RING - HOPS :, :2]))

    free = RING - HOPS
    scale_one, scale_two = 1.0 / math.sqrt(HD), 1.0 / HD
    tile_pairs = rows * rows * (HOPS + 1)
    done = []
    for h in range(heads):
        later, tail = call(
            functools.partial(first_free, scale_one), (shape(free), shape(HOPS)), (info, kvs[h]), free * tile_pairs, 1
        )
        halo_two = from_ring_before(tail)
        mine, split = gains[:, h], h == heads - 1
        pair = lambda n: [pltpu.VMEM((n, rows, HD), BF)] * 2
        known = ()
        if split:
            part = (RING - 2 * HOPS) * tile_pairs
            body = functools.partial(ahead, scale_two)
            known = (call(body, shape(RING - 2 * HOPS), (info, later, mine), part, 1, pair(RING)),)
        early, done_later = call(
            functools.partial(middle, scale_one, scale_two),
            (shape(HOPS), shape(free)),
            (info, kvs[h], halos[h], later, mine, *known),
            RING * tile_pairs,
            1,
            pair(RING),
        )
        done_early = call(
            functools.partial(last, scale_two),
            shape(HOPS if split else RING),
            (info, early, halo_two, mine, *(() if split else (done_later,))),
            HOPS * tile_pairs,
            1,
            pair(2 * HOPS),
        )
        if split:
            sent = [next_section(done_early), next_section(done_later)]
            done.append(exchange(jnp.concatenate(sent, axis=0)))
        else:
            done.append(next_section(exchange(done_early)))
    return call(unpack, jax.ShapeDtypeStruct((rows, width), BF), tuple(done))[None]


def solution(mesh):
    return jax.shard_map(
        program,
        mesh=mesh,
        in_specs=(
            P("section", "ctx", None),
            P("section", "ctx", None),
            P("section", "ctx", None),
            P(),
            P("section", None),
            P("section", None),
        ),
        out_specs=P("section", "ctx", None),
        check_vma=False,
    )
```

```python
import functools
import math

import jax
import jax.numpy as jnp
from jax import lax
from jax.experimental import pallas as pl
from jax.experimental.pallas import tpu as pltpu
from jax.sharding import PartitionSpec as P


HD = 128
HOPS = 3
RING = 8
NEG = -1e30
LOG2E = 1.4426950408889634
BF = jnp.bfloat16
F32 = jnp.float32


def attend(query, keys, values, spot, cut, first, scale, masked):
    rows = query.shape[0]
    row = lax.broadcasted_iota(jnp.int32, (rows, rows), 0)
    col = lax.broadcasted_iota(jnp.int32, (rows, rows), 1)
    own = col <= row

    def score(key):
        return lax.dot_general(query, key, (((1,), (1,)), ((), ())), preferred_element_type=F32)

    parts = [score(key) for key in keys]
    if masked:
        pos = spot + lax.broadcasted_iota(jnp.int32, (rows, 1), 0)
        least = jnp.where(pos >= cut, cut, first)
        for j in range(HOPS + 1):
            begin = spot + (j - HOPS) * rows
            parts[j] = jnp.where(col >= least - begin, parts[j], NEG)
    tiles = [jnp.where(own, parts[HOPS], parts[0])] + parts[1:HOPS]
    peak = tiles[0]
    for tile in tiles[1:]:
        peak = jnp.maximum(peak, tile)
    peak = jnp.max(peak, axis=1, keepdims=True)
    factor = scale * LOG2E
    probs = [jnp.exp2((tile - peak) * factor) for tile in tiles]
    total = probs[0]
    for prob in probs[1:]:
        total = total + prob
    total = jnp.sum(total, axis=1, keepdims=True)
    rounded = [prob.astype(BF) for prob in probs]
    none = jnp.zeros_like(rounded[0])
    weights = [jnp.where(own, none, rounded[0])] + rounded[1:] + [jnp.where(own, rounded[0], none)]
    summed = jnp.zeros((rows, HD), F32)
    for weight, value in zip(weights, values):
        summed = summed + jnp.dot(weight, value, preferred_element_type=F32)
    return (summed / total).astype(BF)


def either(info, spot, rows, run):
    cut, first = info[0], info[1]
    low = spot - HOPS * rows
    need = ((cut > low) & (cut < spot + rows)) | (first > low)

    @pl.when(need)
    def _():
        run(True)

    @pl.when(jnp.logical_not(need))
    def _():
        run(False)


def normalize(block):
    wide = block.astype(F32)
    square = jnp.mean(wide * wide, axis=1, keepdims=True)
    return (wide * lax.rsqrt(square + 1e-06)).astype(BF)


def rows_of(ref):
    return ref.shape[-2]


def first_free(scale, info, kv, out, tail):
    blocks, rows = kv.shape[0], rows_of(kv)

    def step(b, _):
        spot = b * rows

        def run(masked):
            keys = [kv[b - HOPS + j, 0] for j in range(HOPS + 1)]
            values = [kv[b - HOPS + j, 1] for j in range(HOPS + 1)]
            got = attend(kv[b, 2], keys, values, spot, info[0], info[1], scale, masked)
            out[b - HOPS] = normalize(got)

        either(info, spot, rows, run)
        return 0

    lax.fori_loop(HOPS, blocks, step, 0)
    for j in range(HOPS):
        tail[j] = out[out.shape[0] - HOPS + j]


def gained(block, gain):
    return (block.astype(F32) * gain.astype(F32)).astype(BF)


def finish(second, normed):
    return (second.astype(F32) + normed.astype(F32)).astype(BF)


def second_layer(b, scale, info, normed, key_two, gains, write):
    rows = rows_of(normed)
    spot = b * rows

    def run(masked):
        keys = [key_two[b - HOPS + j] for j in range(HOPS + 1)]
        values = [normed[b - HOPS + j] for j in range(HOPS + 1)]
        got = attend(gained(normed[b], gains[0]), keys, values, spot, info[0], info[1], scale, masked)
        write(finish(got, normed[b]))

    either(info, spot, rows, run)


def ahead(scale, info, later, gains, out, normed, key_two):
    count = later.shape[0]
    for b in range(count):
        normed[HOPS + b] = later[b]
        key_two[HOPS + b] = gained(later[b], gains[1])

    def step(b, _):
        def write(block):
            out[b - 2 * HOPS] = block

        second_layer(b, scale, info, normed, key_two, gains, write)
        return 0

    lax.fori_loop(2 * HOPS, HOPS + count, step, 0)


def middle(scale_one, scale_two, info, kv, halo, later, gains, *rest):
    *known, early, out, normed, key_two = rest
    blocks, rows = kv.shape[0], rows_of(kv)
    stop = 2 * HOPS if known else blocks
    for b in range(HOPS):
        spot = b * rows

        def run(masked):
            def pick(t):
                return [halo[j, t] for j in range(b, HOPS)] + [kv[j, t] for j in range(b + 1)]

            got = attend(kv[b, 2], pick(0), pick(1), spot, info[0], info[1], scale_one, masked)
            early[b] = normalize(got)

        either(info, spot, rows, run)
    for b in range(stop):
        block = early[b] if b < HOPS else later[b - HOPS]
        normed[b] = block
        key_two[b] = gained(block, gains[1])

    def step(b, _):
        def write(block):
            out[b - HOPS] = block

        second_layer(b, scale_two, info, normed, key_two, gains, write)
        return 0

    lax.fori_loop(HOPS, stop, step, 0)
    for b in range(stop, blocks):
        out[b - HOPS] = known[0][b - stop]


def last(scale, info, early, halo, gains, *rest):
    *later, out, normed, key_two = rest
    last_blocks(scale, info, early, later, halo, gains, out, normed, key_two)


def last_blocks(scale, info, early, later, halo, gains, out, normed, key_two):
    rows = rows_of(early)
    for j in range(HOPS):
        normed[j] = halo[j]
        normed[HOPS + j] = early[j]
    for j in range(2 * HOPS):
        key_two[j] = gained(normed[j], gains[1])

    def step(b, _):
        spot = b * rows

        def run(masked):
            mine = normed[b + HOPS]
            keys = [key_two[b + j] for j in range(HOPS + 1)]
            values = [normed[b + j] for j in range(HOPS + 1)]
            got = attend(gained(mine, gains[0]), keys, values, spot, info[0], info[1], scale, masked)
            out[b] = finish(got, mine)

        either(info, spot, rows, run)
        return 0

    lax.fori_loop(0, HOPS, step, 0)
    for known in later:
        for j in range(known.shape[0]):
            out[HOPS + j] = known[j]


def pack(h, heads, keys, values, queries, out, held, in_sem, out_sem):
    def load(r, t):
        source = (keys, values, queries)[t]
        at = pl.ds((r * heads + h) * HD, HD)
        return pltpu.make_async_copy(source.at[:, at], held.at[r, t], in_sem.at[r, t])

    def store(r):
        return pltpu.make_async_copy(held.at[r], out.at[r], out_sem.at[r])

    for r in range(RING):
        for t in range(3):
            load(r, t).start()
    for r in range(RING):
        for t in range(3):
            load(r, t).wait()
        store(r).start()
    for r in range(RING):
        store(r).wait()


def packed(h, heads, keys, values, queries):
    rows = keys.shape[0]
    block = (RING, 3, rows, HD)
    anywhere = pl.BlockSpec(memory_space=pl.ANY)
    return pl.pallas_call(
        functools.partial(pack, h, heads),
        out_shape=jax.ShapeDtypeStruct(block, BF),
        in_specs=[anywhere] * 3,
        out_specs=anywhere,
        scratch_shapes=[pltpu.VMEM(block, BF), pltpu.SemaphoreType.DMA((RING, 3)), pltpu.SemaphoreType.DMA((RING,))],
        cost_estimate=pl.CostEstimate(flops=0, bytes_accessed=RING * 3 * rows * HD * 4, transcendentals=0),
    )(keys, values, queries)


def place(where, segments, info):
    ones = jnp.sum(segments[pl.ds(where[0], 1), :])
    info[0] = segments.shape[1] - ones - where[1]
    info[1] = -where[1]


def placed(where, segments):
    return pl.pallas_call(
        place,
        out_shape=jax.ShapeDtypeStruct((2,), jnp.int32),
        in_specs=[pl.BlockSpec(memory_space=pltpu.SMEM), pl.BlockSpec(memory_space=pltpu.VMEM)],
        out_specs=pl.BlockSpec(memory_space=pltpu.SMEM),
        cost_estimate=pl.CostEstimate(flops=0, bytes_accessed=segments.size * 4, transcendentals=0),
        name="place",
    )(where, segments)


def unpack(*refs):
    ins, out = refs[:-1], refs[-1]
    for h, block in enumerate(ins):
        for r in range(RING):
            at = (r * len(ins) + h) * HD
            out[:, at : at + HD] = block[r]


def call(body, out_shape, operands, pairs=0, scalars=0, scratch=()):
    return call_kernel(body, out_shape, operands, pairs, scalars, scratch)


def call_kernel(body, out_shape, operands, pairs, scalars, scratch):
    whole = pl.BlockSpec(memory_space=pltpu.VMEM)
    outs = jax.tree.leaves(out_shape)
    moved = sum(o.size * 2 for o in [*operands[scalars:], *outs])
    return pl.pallas_call(
        body,
        out_shape=out_shape,
        in_specs=[pl.BlockSpec(memory_space=pltpu.SMEM)] * scalars + [whole] * (len(operands) - scalars),
        out_specs=jax.tree.map(lambda _: whole, out_shape),
        scratch_shapes=list(scratch),
        cost_estimate=pl.CostEstimate(flops=pairs * HD * 4, bytes_accessed=moved, transcendentals=pairs),
        compiler_params=pltpu.CompilerParams(vmem_limit_bytes=40 << 20),
    )(*operands)


def program(queries, keys, values, segments, gain_query, gain_key):
    section, sections = lax.axis_index("section"), lax.axis_size("section")
    ctx, ctxs = lax.axis_index("ctx"), lax.axis_size("ctx")
    rows, width = queries.shape[1], queries.shape[2]
    heads = width // HD // RING
    rings = [list(range(r * RING, r * RING + RING)) for r in range(ctxs // RING)]

    def exchange(block):
        return lax.all_to_all(block, "ctx", 0, 0, axis_index_groups=rings)

    def from_ring_before(block):
        return lax.ppermute(block, "ctx", [(i, i + RING) for i in range(ctxs - RING)])

    def next_section(block):
        return lax.ppermute(block, "section", [(i, (i + 1) % sections) for i in range(sections)])

    def shape(*dims):
        return jax.ShapeDtypeStruct((*dims, rows, HD), BF)

    where = jnp.stack([section, (ctx // RING) * (RING * rows)]).astype(jnp.int32)
    ready = [packed(h, heads, keys[0], values[0], queries[0]) for h in range(heads)]
    info = placed(where, segments)
    gains = jnp.concatenate([gain_query, gain_key], axis=0)
    gains = lax.ppermute(gains, "section", [((i + 1) % sections, i) for i in range(sections)])
    gains = lax.dynamic_slice_in_dim(gains, (ctx % RING) * heads * HD, heads * HD, 1).reshape(2, heads, 1, HD)

    kvs, halos = [], []
    for h in range(heads):
        kv = exchange(ready[h])
        kvs.append(kv)
        halos.append(from_ring_before(kv[RING - HOPS :, :2]))

    free = RING - HOPS
    scale_one, scale_two = 1.0 / math.sqrt(HD), 1.0 / HD
    tile_pairs = rows * rows * (HOPS + 1)
    done = []
    for h in range(heads):
        later, tail = call(
            functools.partial(first_free, scale_one), (shape(free), shape(HOPS)), (info, kvs[h]), free * tile_pairs, 1
        )
        halo_two = from_ring_before(tail)
        mine, split = gains[:, h], h == heads - 1
        pair = lambda n: [pltpu.VMEM((n, rows, HD), BF)] * 2
        known = ()
        if split:
            part = (RING - 2 * HOPS) * tile_pairs
            body = functools.partial(ahead, scale_two)
            known = (call(body, shape(RING - 2 * HOPS), (info, later, mine), part, 1, pair(RING)),)
        early, done_later = call(
            functools.partial(middle, scale_one, scale_two),
            (shape(HOPS), shape(free)),
            (info, kvs[h], halos[h], later, mine, *known),
            RING * tile_pairs,
            1,
            pair(RING),
        )
        done_early = call(
            functools.partial(last, scale_two),
            shape(HOPS if split else RING),
            (info, early, halo_two, mine, *(() if split else (done_later,))),
            HOPS * tile_pairs,
            1,
            pair(2 * HOPS),
        )
        if split:
            sent = [next_section(done_early), next_section(done_later)]
            done.append(exchange(jnp.concatenate(sent, axis=0)))
        else:
            done.append(next_section(exchange(done_early)))
    return call(unpack, jax.ShapeDtypeStruct((rows, width), BF), tuple(done))[None]


def solution(mesh):
    return jax.shard_map(
        program,
        mesh=mesh,
        in_specs=(
            P("section", "ctx", None),
            P("section", "ctx", None),
            P("section", "ctx", None),
            P(),
            P("section", None),
            P("section", None),
        ),
        out_specs=P("section", "ctx", None),
        check_vma=False,
    )
```

```python
import functools
import math

import jax
import jax.numpy as jnp
from jax import lax
from jax.experimental import pallas as pl
from jax.experimental.pallas import tpu as pltpu
from jax.sharding import PartitionSpec as P


HD = 128
HOPS = 3
RING = 8
NEG = -1e30
LOG2E = 1.4426950408889634
BF = jnp.bfloat16
F32 = jnp.float32


def attend(query, keys, values, spot, cut, first, scale, masked):
    rows = query.shape[0]
    row = lax.broadcasted_iota(jnp.int32, (rows, rows), 0)
    col = lax.broadcasted_iota(jnp.int32, (rows, rows), 1)
    own = col <= row

    def score(key):
        return lax.dot_general(query, key, (((1,), (1,)), ((), ())), preferred_element_type=F32)

    parts = [score(key) for key in keys]
    if masked:
        pos = spot + lax.broadcasted_iota(jnp.int32, (rows, 1), 0)
        least = jnp.where(pos >= cut, cut, first)
        for j in range(HOPS + 1):
            begin = spot + (j - HOPS) * rows
            parts[j] = jnp.where(col >= least - begin, parts[j], NEG)
    tiles = [jnp.where(own, parts[HOPS], parts[0])] + parts[1:HOPS]
    peak = tiles[0]
    for tile in tiles[1:]:
        peak = jnp.maximum(peak, tile)
    peak = jnp.max(peak, axis=1, keepdims=True)
    factor = scale * LOG2E
    probs = [jnp.exp2((tile - peak) * factor) for tile in tiles]
    total = probs[0]
    for prob in probs[1:]:
        total = total + prob
    total = jnp.sum(total, axis=1, keepdims=True)
    rounded = [prob.astype(BF) for prob in probs]
    none = jnp.zeros_like(rounded[0])
    weights = [jnp.where(own, none, rounded[0])] + rounded[1:] + [jnp.where(own, rounded[0], none)]
    summed = jnp.zeros((rows, HD), F32)
    for weight, value in zip(weights, values):
        summed = summed + jnp.dot(weight, value, preferred_element_type=F32)
    return (summed / total).astype(BF)


def either(info, spot, rows, run, count=1):
    cut, first = info[0], info[1]
    low = spot - HOPS * rows
    need = ((cut > low) & (cut < spot + count * rows)) | (first > low)

    @pl.when(need)
    def _():
        run(True)

    @pl.when(jnp.logical_not(need))
    def _():
        run(False)


def normalize(block):
    wide = block.astype(F32)
    square = jnp.mean(wide * wide, axis=1, keepdims=True)
    return (wide * lax.rsqrt(square + 1e-06)).astype(BF)


def rows_of(ref):
    return ref.shape[-2]


def first_free(scale, info, kv, out, tail):
    blocks, rows = kv.shape[0], rows_of(kv)

    def step(b, _):
        spot = b * rows

        def run(masked):
            keys = [kv[b - HOPS + j, 0] for j in range(HOPS + 1)]
            values = [kv[b - HOPS + j, 1] for j in range(HOPS + 1)]
            got = attend(kv[b, 2], keys, values, spot, info[0], info[1], scale, masked)
            out[b - HOPS] = normalize(got)

        either(info, spot, rows, run)
        return 0

    lax.fori_loop(HOPS, blocks, step, 0)
    for j in range(HOPS):
        tail[j] = out[out.shape[0] - HOPS + j]


def gained(block, gain):
    return (block.astype(F32) * gain.astype(F32)).astype(BF)


def finish(second, normed):
    return (second.astype(F32) + normed.astype(F32)).astype(BF)


def second_layer(b, scale, info, normed, key_two, gains, write, count=1):
    rows = rows_of(normed)

    def run(masked):
        for at in [b + i for i in range(count)]:
            keys = [key_two[at - HOPS + j] for j in range(HOPS + 1)]
            values = [normed[at - HOPS + j] for j in range(HOPS + 1)]
            query = gained(normed[at], gains[0])
            got = attend(query, keys, values, at * rows, info[0], info[1], scale, masked)
            write(at, finish(got, normed[at]))

    either(info, b * rows, rows, run, count)


def ahead(scale, info, later, gains, out, normed, key_two):
    count = later.shape[0]
    for b in range(count):
        normed[HOPS + b] = later[b]
        key_two[HOPS + b] = gained(later[b], gains[1])

    def step(b):
        def write(at, block):
            out[at - 2 * HOPS] = block

        second_layer(b, scale, info, normed, key_two, gains, write, count - HOPS)
        return 0

    step(2 * HOPS)


def middle(scale_one, scale_two, info, kv, halo, later, gains, *rest):
    *known, early, out, normed, key_two = rest
    blocks, rows = kv.shape[0], rows_of(kv)
    stop = 2 * HOPS if known else blocks

    def first_blocks(masked):
        for b in range(HOPS):

            def pick(t):
                return [halo[j, t] for j in range(b, HOPS)] + [kv[j, t] for j in range(b + 1)]

            got = attend(kv[b, 2], pick(0), pick(1), b * rows, info[0], info[1], scale_one, masked)
            early[b] = normalize(got)

    either(info, 0, rows, first_blocks, HOPS)
    for b in range(stop):
        block = early[b] if b < HOPS else later[b - HOPS]
        normed[b] = block
        key_two[b] = gained(block, gains[1])

    def step(b, count):
        def write(at, block):
            out[at - HOPS] = block

        second_layer(b, scale_two, info, normed, key_two, gains, write, count)

    if known:
        step(HOPS, HOPS)
    else:
        lax.fori_loop(HOPS, stop, lambda b, _: step(b, 1) or 0, 0)
    for b in range(stop, blocks):
        out[b - HOPS] = known[0][b - stop]


def last(scale, info, early, halo, gains, *rest):
    *later, out, normed, key_two = rest
    last_blocks(scale, info, early, later, halo, gains, out, normed, key_two)


def last_blocks(scale, info, early, later, halo, gains, out, normed, key_two):
    rows = rows_of(early)
    for j in range(HOPS):
        normed[j] = halo[j]
        normed[HOPS + j] = early[j]
    for j in range(2 * HOPS):
        key_two[j] = gained(normed[j], gains[1])

    def run(masked):
        for b in range(HOPS):
            mine = normed[b + HOPS]
            keys = [key_two[b + j] for j in range(HOPS + 1)]
            values = [normed[b + j] for j in range(HOPS + 1)]
            got = attend(gained(mine, gains[0]), keys, values, b * rows, info[0], info[1], scale, masked)
            out[b] = finish(got, mine)

    either(info, 0, rows, run, HOPS)
    for known in later:
        for j in range(known.shape[0]):
            out[HOPS + j] = known[j]


def pack(h, heads, keys, values, queries, out, held, in_sem, out_sem):
    def load(r, t):
        source = (keys, values, queries)[t]
        at = pl.ds((r * heads + h) * HD, HD)
        return pltpu.make_async_copy(source.at[:, at], held.at[r, t], in_sem.at[r, t])

    def store(r):
        return pltpu.make_async_copy(held.at[r], out.at[r], out_sem.at[r])

    for r in range(RING):
        for t in range(3):
            load(r, t).start()
    for r in range(RING):
        for t in range(3):
            load(r, t).wait()
        store(r).start()
    for r in range(RING):
        store(r).wait()


def packed(h, heads, keys, values, queries):
    rows = keys.shape[0]
    block = (RING, 3, rows, HD)
    anywhere = pl.BlockSpec(memory_space=pl.ANY)
    return pl.pallas_call(
        functools.partial(pack, h, heads),
        out_shape=jax.ShapeDtypeStruct(block, BF),
        in_specs=[anywhere] * 3,
        out_specs=anywhere,
        scratch_shapes=[pltpu.VMEM(block, BF), pltpu.SemaphoreType.DMA((RING, 3)), pltpu.SemaphoreType.DMA((RING,))],
        cost_estimate=pl.CostEstimate(flops=0, bytes_accessed=RING * 3 * rows * HD * 4, transcendentals=0),
    )(keys, values, queries)


def place(where, segments, info):
    ones = jnp.sum(segments[pl.ds(where[0], 1), :])
    info[0] = segments.shape[1] - ones - where[1]
    info[1] = -where[1]


def placed(where, segments):
    return pl.pallas_call(
        place,
        out_shape=jax.ShapeDtypeStruct((2,), jnp.int32),
        in_specs=[pl.BlockSpec(memory_space=pltpu.SMEM), pl.BlockSpec(memory_space=pltpu.VMEM)],
        out_specs=pl.BlockSpec(memory_space=pltpu.SMEM),
        cost_estimate=pl.CostEstimate(flops=0, bytes_accessed=segments.size * 4, transcendentals=0),
        name="place",
    )(where, segments)


def unpack(*refs):
    ins, out = refs[:-1], refs[-1]
    for h, block in enumerate(ins):
        for r in range(RING):
            at = (r * len(ins) + h) * HD
            out[:, at : at + HD] = block[r]


def call(body, out_shape, operands, pairs=0, scalars=0, scratch=()):
    return call_kernel(body, out_shape, operands, pairs, scalars, scratch)


def call_kernel(body, out_shape, operands, pairs, scalars, scratch):
    whole = pl.BlockSpec(memory_space=pltpu.VMEM)
    outs = jax.tree.leaves(out_shape)
    moved = sum(o.size * 2 for o in [*operands[scalars:], *outs])
    return pl.pallas_call(
        body,
        out_shape=out_shape,
        in_specs=[pl.BlockSpec(memory_space=pltpu.SMEM)] * scalars + [whole] * (len(operands) - scalars),
        out_specs=jax.tree.map(lambda _: whole, out_shape),
        scratch_shapes=list(scratch),
        cost_estimate=pl.CostEstimate(flops=pairs * HD * 4, bytes_accessed=moved, transcendentals=pairs),
        compiler_params=pltpu.CompilerParams(vmem_limit_bytes=40 << 20),
    )(*operands)


def program(queries, keys, values, segments, gain_query, gain_key):
    section, sections = lax.axis_index("section"), lax.axis_size("section")
    ctx, ctxs = lax.axis_index("ctx"), lax.axis_size("ctx")
    rows, width = queries.shape[1], queries.shape[2]
    heads = width // HD // RING
    rings = [list(range(r * RING, r * RING + RING)) for r in range(ctxs // RING)]

    def exchange(block):
        return lax.all_to_all(block, "ctx", 0, 0, axis_index_groups=rings)

    def from_ring_before(block):
        return lax.ppermute(block, "ctx", [(i, i + RING) for i in range(ctxs - RING)])

    def next_section(block):
        return lax.ppermute(block, "section", [(i, (i + 1) % sections) for i in range(sections)])

    def shape(*dims):
        return jax.ShapeDtypeStruct((*dims, rows, HD), BF)

    where = jnp.stack([section, (ctx // RING) * (RING * rows)]).astype(jnp.int32)
    ready = [packed(h, heads, keys[0], values[0], queries[0]) for h in range(heads)]
    info = placed(where, segments)
    gains = jnp.concatenate([gain_query, gain_key], axis=0)
    gains = lax.ppermute(gains, "section", [((i + 1) % sections, i) for i in range(sections)])
    gains = lax.dynamic_slice_in_dim(gains, (ctx % RING) * heads * HD, heads * HD, 1).reshape(2, heads, 1, HD)

    kvs, halos = [], []
    for h in range(heads):
        kv = exchange(ready[h])
        kvs.append(kv)
        halos.append(from_ring_before(kv[RING - HOPS :, :2]))

    free = RING - HOPS
    scale_one, scale_two = 1.0 / math.sqrt(HD), 1.0 / HD
    tile_pairs = rows * rows * (HOPS + 1)
    done = []
    for h in range(heads):
        later, tail = call(
            functools.partial(first_free, scale_one), (shape(free), shape(HOPS)), (info, kvs[h]), free * tile_pairs, 1
        )
        halo_two = from_ring_before(tail)
        mine, split = gains[:, h], h == heads - 1
        pair = lambda n: [pltpu.VMEM((n, rows, HD), BF)] * 2
        known = ()
        if split:
            part = (RING - 2 * HOPS) * tile_pairs
            body = functools.partial(ahead, scale_two)
            known = (call(body, shape(RING - 2 * HOPS), (info, later, mine), part, 1, pair(RING)),)
        early, done_later = call(
            functools.partial(middle, scale_one, scale_two),
            (shape(HOPS), shape(free)),
            (info, kvs[h], halos[h], later, mine, *known),
            RING * tile_pairs,
            1,
            pair(RING),
        )
        done_early = call(
            functools.partial(last, scale_two),
            shape(HOPS if split else RING),
            (info, early, halo_two, mine, *(() if split else (done_later,))),
            HOPS * tile_pairs,
            1,
            pair(2 * HOPS),
        )
        if split:
            sent = [next_section(done_early), next_section(done_later)]
            done.append(exchange(jnp.concatenate(sent, axis=0)))
        else:
            done.append(next_section(exchange(done_early)))
    return call(unpack, jax.ShapeDtypeStruct((rows, width), BF), tuple(done))[None]


def solution(mesh):
    return jax.shard_map(
        program,
        mesh=mesh,
        in_specs=(
            P("section", "ctx", None),
            P("section", "ctx", None),
            P("section", "ctx", None),
            P(),
            P("section", None),
            P("section", None),
        ),
        out_specs=P("section", "ctx", None),
        check_vma=False,
    )
```
